1024 devices in a mesh: dp: 4 (over z_lo), tp: 256 (over y, x, z_hi, core).
Axes of the slice: x: 4, y: 8, z: 16 (z_hi: 4, z_lo: 4; z = z_hi * 4 + z_lo), core: 2. Of those that a mesh axis runs over, the one named last changes fastest.
Arguments:
- hidden: bfloat16 [1024, 26624], P('dp', 'tp'), may hold values from -0.1875 to 0.1875
- out_grad: bfloat16 [1024, 8192], P(('dp', 'tp')), may hold values from -6 to 6
- down_weight: bfloat16 [26624, 8192], P('tp', 'dp'), may hold values from -0.0625 to 0.0625
Outputs:
- input_grad: bfloat16 [1024, 26624], P('dp', 'tp')
- weight_grad: bfloat16 [26624, 8192], P('tp', 'dp')
The draws below stay inside these ranges and needn't reach their ends.
All inputs are finite; a program needn't handle non-finite values.
Results may differ from the reference program's by a relative error of at most 0.009.
Values may be sent and summed in bfloat16 or wider, within the bound.
No kernel may reach another device: no remote copies, remote signals or barrier semaphores. Data moves between devices by JAX's collectives and lax.ppermute only.
A program may use at most 32 MiB of HBM per device.

```python
import jax
import jax.numpy as jnp

D = 8192
FF = 26624
TOK_DEV = 256
TOKENS = 1024
N_DP = 4


def block_levels(key, shape, cuts, low, top_value):
    gain = 1.0
    for dim, blocks in cuts:
        draws = jax.random.uniform(jax.random.fold_in(jax.random.fold_in(key, 6), dim), (blocks,), jnp.float32, low / len(cuts), top_value / len(cuts))
        gain = gain * jnp.repeat(jnp.exp(draws), shape[dim] // blocks).reshape((-1,) + (1,) * (len(shape) - 1 - dim))
    return gain


def scatter_about(stream_key, shape, width, bound, pieces=(), dtype=jnp.bfloat16):
    result = jax.random.normal(stream_key, shape, jnp.float32) * width
    if len(pieces) > 0:
        result = block_levels(stream_key, shape, pieces, -0.22, 0.18) * result
    return jnp.clip(result, min=-bound, max=bound).astype(dtype)


def setup_inputs(seed: int = 0) -> dict:
    key_of = jax.random.split(jax.random.key(seed), 4)
    hidden = scatter_about(key_of[0], (TOKENS, FF), TOKENS ** -0.5, 0.1875, ((0, 4), (1, 256)))
    out_grad = scatter_about(key_of[1], (TOKENS, D), 1.0, 6.0, ((0, 1024),))
    down_weight = scatter_about(key_of[2], (FF, D), D ** -0.5, 0.0625, ((0, 256), (1, 4)))
    return dict(hidden=hidden, out_grad=out_grad, down_weight=down_weight)


def reference(hidden, out_grad, down_weight):
    input_grad = jnp.dot(out_grad, down_weight.T, preferred_element_type=jnp.float32).astype(jnp.bfloat16)
    summed = jnp.zeros((FF, D), jnp.float32)
    for group in range(N_DP):
        first = group * TOK_DEV
        hidden_group = hidden[first:first + TOK_DEV]
        grad_group = out_grad[first:first + TOK_DEV]
        partial_grad = jnp.dot(hidden_group.T, grad_group, preferred_element_type=jnp.float32).astype(jnp.bfloat16)
        summed = summed + partial_grad.astype(jnp.float32)
    return input_grad, summed.astype(jnp.bfloat16)
```

```python
import numpy as np

import jax
import jax.numpy as jnp
from jax import lax
from jax.sharding import Mesh, PartitionSpec as P


BF16, F32 = jnp.bfloat16, jnp.float32
DP, Y, X, ZH, CORE = 4, 8, 4, 4, 2
ROWS = X * DP * ZH


def ring_pairs():
    pairs = []
    for y in range(Y):
        pairs.append((y * CORE, ((y + 1) % Y) * CORE))
        pairs.append((y * CORE + 1, ((y - 1) % Y) * CORE + 1))
    return pairs


SWAP = [(0, 1), (1, 0)]


def arrival_to_group():
    chunks = 8
    order = np.arange(chunks * ROWS).reshape(chunks, X, DP, ZH).transpose(2, 0, 1, 3).ravel()
    hot = np.zeros((chunks * ROWS, chunks * ROWS), np.float32)
    hot[order, np.arange(chunks * ROWS)] = 1
    return hot


GROUPED = arrival_to_group()
CHUNKS = [(0, 0), (1, 0), (1, 1), (2, 0), (2, 1), (3, 0), (3, 1), (4, 0)]


def token_order(y):
    step = np.array([s for s, _ in CHUNKS])
    flip = np.array([f for _, f in CHUNKS])
    core = np.arange(CORE)
    sign = np.array([-1, 1])
    local = (np.arange(X)[:, None] * 8 + np.arange(ZH)[None, :] * 2).ravel()
    offset = (sign[:, None] * step[None, :]).reshape(-1)
    which = (core[:, None] ^ flip[None, :]).reshape(-1)
    row = jnp.mod(y + jnp.asarray(offset, jnp.int32) + Y, Y) * 32 + jnp.asarray(which, jnp.int32)
    return (row[:, None] + jnp.asarray(local, jnp.int32)[None, :]).reshape(-1)


def dot(a, b, ca, cb):
    return lax.dot_general(a, b, (((ca,), (cb,)), ((), ())), preferred_element_type=F32)


def shards(hidden, out_grad, down_weight):
    ff, width = down_weight.shape
    me = lax.axis_index("core")
    y = lax.axis_index("y")

    row = jnp.broadcast_to(out_grad.reshape(DP, 1, width), (DP, ZH, width)).reshape(DP * ZH, width)
    mine = lax.all_to_all(row, ("dp", "zh"), 0, 0, tiled=True)
    spread = jnp.broadcast_to(mine[None], (X, DP * ZH, width))
    u0 = lax.all_to_all(spread, "x", 0, 0, tiled=True).reshape(ROWS, width)

    pairs = ring_pairs()
    u1 = lax.ppermute(u0, ("y", "core"), pairs)
    v0 = lax.ppermute(u0, "core", SWAP)
    v1 = lax.ppermute(v0, ("y", "core"), pairs)
    u2 = lax.ppermute(u1, ("y", "core"), pairs)
    v2 = lax.ppermute(v1, ("y", "core"), pairs)
    u3 = lax.ppermute(u2, ("y", "core"), pairs)
    v3 = lax.ppermute(v2, ("y", "core"), pairs)
    u4 = lax.ppermute(u3, ("y", "core"), pairs)

    order = token_order(y)
    hot = (lax.broadcasted_iota(jnp.int32, (256, 256), 0) == order[None, :]).astype(BF16)
    ordered = dot(hidden, hot, 0, 0).astype(BF16)
    halves = ordered.reshape(ff, CORE, 128).transpose(1, 0, 2)
    sent = jnp.broadcast_to(halves[None], (DP, CORE, ff, 128)).reshape(DP * CORE, ff, 128)
    got = lax.all_to_all(sent, ("dp", "core"), 0, 0, tiled=True).reshape(DP, CORE, ff, 128)
    units = got.transpose(1, 2, 0, 3).reshape(CORE * ff, DP * 128)
    grouped = jnp.asarray(GROUPED, BF16)
    units = dot(units, grouped, 1, 1).astype(BF16)

    other = lax.ppermute(down_weight, "core", SWAP)
    first = jnp.where(me == 0, down_weight, other)
    second = jnp.where(me == 0, other, down_weight)
    weight = jnp.concatenate([first, second], axis=0)

    early = jnp.concatenate([u0, u1, v1, u2, v2, u3], axis=0)
    late = jnp.concatenate([v3, u4], axis=0)
    n = early.shape[0]
    grad_w = dot(units[:, :n], early, 1, 0)
    ig_early = dot(weight, early, 1, 1).astype(BF16)
    grad_w = grad_w + dot(units[:, n:], late, 1, 0)
    ig_late = dot(weight, late, 1, 1).astype(BF16)

    keep = lax.dynamic_slice_in_dim(grad_w, me * ff, ff, 0)
    give = lax.dynamic_slice_in_dim(grad_w, (1 - me) * ff, ff, 0).astype(BF16)
    taken = lax.ppermute(give, "core", SWAP)

    parts = jnp.concatenate([ig_early, ig_late], axis=1)
    parts = dot(parts, grouped, 1, 0).astype(BF16).reshape(CORE, ff, DP, 128)
    parts = parts.transpose(2, 0, 1, 3).reshape(DP * CORE, ff, 128)
    back = lax.all_to_all(parts, ("dp", "core"), 0, 0, tiled=True).reshape(DP, CORE, ff, 128)
    summed = jnp.sum(back.astype(F32), axis=0).astype(BF16)
    summed = summed.transpose(1, 0, 2).reshape(ff, 256)
    input_grad = dot(hot, summed, 1, 1).astype(BF16)

    weight_grad = (keep + taken.astype(F32)).astype(BF16)
    return input_grad, weight_grad


def solution(mesh):
    fine = Mesh(mesh.devices.reshape(DP, Y, X, ZH, CORE), ("dp", "y", "x", "zh", "core"))
    tp = ("y", "x", "zh", "core")
    return jax.shard_map(
        shards,
        mesh=fine,
        in_specs=(P("dp", tp), P(("dp",) + tp, None), P(tp, "dp")),
        out_specs=(P("dp", tp), P(tp, "dp")),
        check_vma=False,
    )
```

```python
import functools

import jax
import jax.numpy as jnp
from jax import lax
from jax.experimental import pallas as pl
from jax.experimental.pallas import tpu as pltpu
from jax.sharding import Mesh, PartitionSpec as P


BF16, F32 = jnp.bfloat16, jnp.float32
DP, Y, X, ZH, CORE = 4, 8, 4, 4, 2
ROWS = X * DP * ZH
CHUNKS = 8
EARLY = 6
TOK = 256
HALF = TOK // CORE
VMEM = pl.BlockSpec(memory_space=pltpu.VMEM)
SMEM = pl.BlockSpec(memory_space=pltpu.SMEM)
SWAP = [(0, 1), (1, 0)]


def ring_pairs(cross):
    pairs = []
    for y in range(Y):
        for core, way in ((0, 1), (1, -1)):
            pairs.append((y * CORE + (core ^ cross), ((y + way) % Y) * CORE + core))
    return pairs


def dot(a, b, ca, cb):
    return lax.dot_general(a, b, (((ca,), (cb,)), ((), ())), preferred_element_type=F32)


def call(body, outs, *args, flops=0, aliases=None):
    outs = [jax.ShapeDtypeStruct(s, d) for s, d in outs]
    moved = sum(a.size * a.dtype.itemsize for a in args) + sum(o.size * o.dtype.itemsize for o in outs)
    specs = [SMEM if a.dtype == jnp.int32 else VMEM for a in args]
    return pl.pallas_call(
        body,
        out_shape=outs,
        in_specs=specs,
        out_specs=[VMEM] * len(outs),
        input_output_aliases=aliases or {},
        cost_estimate=pl.CostEstimate(flops=flops, bytes_accessed=moved, transcendentals=0),
        compiler_params=pltpu.CompilerParams(vmem_limit_bytes=12 * 2**20),
    )(*args)


def token_at(p, y):
    core, q, x, zh = p >> 7, (p >> 4) & 7, (p >> 2) & 3, p & 3
    step = (q + 1) >> 1
    flip = jnp.where(((q & 1) == 0) & (q > 0), 1, 0)
    row = (y + jnp.where(core == 0, -step, step)) & 7
    return row * 32 + x * 8 + zh * 2 + (core ^ flip)


def iota(shape, dim):
    return lax.broadcasted_iota(jnp.int32, shape, dim)


def hidden_body(at, hidden, sent):
    hot = (iota((TOK, TOK), 0) == token_at(iota((TOK, TOK), 1), at[1])).astype(BF16)
    ordered = dot(hidden[...], hot, 1, 0).astype(BF16)
    for g in range(DP):
        for c in range(CORE):
            sent[g * CORE + c] = ordered[:, c * HALF:(c + 1) * HALF]


def units_body(ff, pad, at, got, mine, other, units, weight, grouped):
    me = at[0]
    a = iota((CHUNKS * ROWS, CHUNKS * ROWS), 0)
    b = iota((CHUNKS * ROWS, CHUNKS * ROWS), 1)
    place = ((a >> 2) & 3) * HALF + (a >> 6) * 16 + ((a >> 4) & 3) * 4 + (a & 3)
    hot = (place == b).astype(BF16)
    grouped[...] = hot
    gap = jnp.zeros((pad - ff, CHUNKS * ROWS), F32)
    rows = []
    for j in range(CORE):
        rows.append(jnp.concatenate([got[g * CORE + (me ^ j)] for g in range(DP)], axis=1))
    for j in range(CORE):
        moved = dot(rows[j], hot, 1, 1)
        units[pl.ds(j * pad, pad)] = jnp.concatenate([moved, gap], axis=0).astype(BF16)
    blank = jnp.zeros((pad - ff, mine.shape[1]), BF16)
    weight[pl.ds(0, ff)] = mine[...]
    weight[pl.ds(ff, pad - ff)] = blank
    weight[pl.ds(pad, ff)] = other[...]
    weight[pl.ds(pad + ff, pad - ff)] = blank


def early_body(units, weight, grouped, *refs):
    chunks, (grad, parts) = refs[:EARLY], refs[EARLY:]
    n = EARLY * ROWS
    width = weight.shape[1]
    inner = jnp.concatenate([c[...] for c in chunks], axis=0)
    ig = dot(weight[...], inner, 1, 1).astype(BF16)
    parts[...] = dot(ig, grouped[pl.ds(0, n)], 1, 0).astype(BF16)
    left = units[:, :n]
    for j in range(0, width, 512):
        cols = jnp.concatenate([c[:, j:j + 512] for c in chunks], axis=0)
        grad[:, j:j + 512] = dot(left, cols, 1, 0)


def parts_body(ff, pad, at, weight, grouped, early, *refs):
    chunks, (out,) = refs[:-1], refs[-1:]
    me = at[0]
    n = EARLY * ROWS
    inner = jnp.concatenate([c[...] for c in chunks], axis=0)
    ig = dot(weight[...], inner, 1, 1).astype(BF16)
    parts = (dot(ig, grouped[pl.ds(n, CHUNKS * ROWS - n)], 1, 0) + early[...].astype(F32)).astype(BF16)
    for g in range(DP):
        for j in range(CORE):
            out[g * CORE + (me ^ j)] = parts[j * pad:j * pad + ff, g * HALF:(g + 1) * HALF]


def late_body(ff, pad, units, grad, *refs):
    chunks, (keep, give) = refs[:-2], refs[-2:]
    n = EARLY * ROWS
    width = grad.shape[1]
    left = units[:, n:]
    for k in range(0, width, 512):
        cols = jnp.concatenate([c[:, k:k + 512] for c in chunks], axis=0)
        total = grad[:, k:k + 512] + dot(left, cols, 1, 0)
        keep[:, k:k + 512] = total[:ff]
        give[:, k:k + 512] = total[pad:pad + ff].astype(BF16)


def final_body(at, back, out):
    hot = (token_at(iota((TOK, TOK), 0), at[1]) == iota((TOK, TOK), 1)).astype(BF16)
    halves = []
    for c in range(CORE):
        total = back[c].astype(F32)
        for g in range(1, DP):
            total = total + back[g * CORE + c].astype(F32)
        halves.append(total.astype(BF16))
    out[...] = dot(jnp.concatenate(halves, axis=1), hot, 1, 0).astype(BF16)


def add_body(keep, taken, out):
    out[...] = (keep[...] + taken[...].astype(F32)).astype(BF16)


def ring(value, cross=0):
    return lax.ppermute(value, ("y", "core"), ring_pairs(cross))


def step(hidden, out_grad, down_weight):
    ff, width = down_weight.shape
    pad = -(-ff // 16) * 16
    at = jnp.stack([lax.axis_index("core"), lax.axis_index("y")]).astype(jnp.int32)

    row = jnp.broadcast_to(out_grad.reshape(DP, 1, 2, width // 2), (DP, ZH, 2, width // 2))
    row = row.reshape(DP * ZH, 2, width // 2)
    mine = lax.all_to_all(row, ("dp", "zh"), 0, 0, tiled=True).reshape(DP * ZH, width)
    spread = jnp.broadcast_to(mine[None], (X, DP * ZH, width))
    u0 = lax.all_to_all(spread, "x", 0, 0, tiled=True).reshape(ROWS, width)

    (sent,) = call(hidden_body, [((DP * CORE, ff, HALF), BF16)], at, hidden.T)
    got = lax.all_to_all(sent, ("dp", "core"), 0, 0, tiled=True)
    other = lax.ppermute(down_weight, "core", SWAP)
    units, weight, grouped = call(
        functools.partial(units_body, ff, pad),
        [((2 * pad, CHUNKS * ROWS), BF16), ((2 * pad, width), BF16), ((CHUNKS * ROWS, CHUNKS * ROWS), BF16)],
        at, got, down_weight, other,
    )

    u1 = ring(u0)
    v1 = ring(u0, cross=1)
    u2 = ring(u1)
    v2 = ring(v1)
    u3 = ring(u2)
    v3 = ring(v2)
    u4 = ring(u3)

    flops = 4 * pad * width * ROWS * CORE
    grad, parts = call(
        early_body, [((2 * pad, width), F32), ((2 * pad, CHUNKS * ROWS), BF16)],
        units, weight, grouped, u0, u1, v1, u2, v2, u3, flops=EARLY * flops,
    )
    (parts,) = call(
        functools.partial(parts_body, ff, pad), [((DP * CORE, ff, HALF), BF16)],
        at, weight, grouped, parts, v3, u4, flops=flops,
    )
    back = lax.all_to_all(parts, ("dp", "core"), 0, 0, tiled=True)
    keep, give = call(
        functools.partial(late_body, ff, pad), [((ff, width), F32), ((ff, width), BF16)],
        units, grad, v3, u4, flops=flops,
    )
    taken = lax.ppermute(give, "core", SWAP)
    (weight_grad,) = call(add_body, [((ff, width), BF16)], keep, taken)
    (input_grad,) = call(final_body, [((ff, TOK), BF16)], at, back)
    return input_grad.T, weight_grad


def solution(mesh):
    fine = Mesh(mesh.devices.reshape(DP, Y, X, ZH, CORE), ("dp", "y", "x", "zh", "core"))
    tp = ("y", "x", "zh", "core")
    return jax.shard_map(
        step,
        mesh=fine,
        in_specs=(P("dp", tp), P(("dp",) + tp, None), P(tp, "dp")),
        out_specs=(P("dp", tp), P(tp, "dp")),
        check_vma=False,
    )
```

```python
import functools

import jax
import jax.numpy as jnp
from jax import lax
from jax.experimental import pallas as pl
from jax.experimental.pallas import tpu as pltpu
from jax.sharding import Mesh, PartitionSpec as P


BF16, F32 = jnp.bfloat16, jnp.float32
DP, Y, X, ZH, CORE = 4, 8, 4, 4, 2
ROWS = X * DP * ZH
CHUNKS = 8
EARLY = 6
TOK = 256
HALF = TOK // CORE
VMEM = pl.BlockSpec(memory_space=pltpu.VMEM)
SMEM = pl.BlockSpec(memory_space=pltpu.SMEM)
SWAP = [(0, 1), (1, 0)]


def ring_pairs(cross):
    pairs = []
    for y in range(Y):
        for core, way in ((0, 1), (1, -1)):
            pairs.append((y * CORE + (core ^ cross), ((y + way) % Y) * CORE + core))
    return pairs


def dot(a, b, ca, cb):
    return lax.dot_general(a, b, (((ca,), (cb,)), ((), ())), preferred_element_type=F32)


def call(body, outs, *args, flops=0, aliases=None):
    outs = [jax.ShapeDtypeStruct(s, d) for s, d in outs]
    moved = sum(a.size * a.dtype.itemsize for a in args) + sum(o.size * o.dtype.itemsize for o in outs)
    specs = [SMEM if a.dtype == jnp.int32 else VMEM for a in args]
    return pl.pallas_call(
        body,
        out_shape=outs,
        in_specs=specs,
        out_specs=[VMEM] * len(outs),
        input_output_aliases=aliases or {},
        cost_estimate=pl.CostEstimate(flops=flops, bytes_accessed=moved, transcendentals=0),
        compiler_params=pltpu.CompilerParams(vmem_limit_bytes=12 * 2**20),
    )(*args)


def token_at(p, y):
    core, q, x, zh = p >> 7, (p >> 4) & 7, (p >> 2) & 3, p & 3
    step = jnp.where(q == 1, 4, q >> 1)
    flip = jnp.where(q == 1, 0, q & 1)
    row = (y + jnp.where(core == 0, -step, step)) & 7
    return row * 32 + x * 8 + zh * 2 + (core ^ flip)


def iota(shape, dim):
    return lax.broadcasted_iota(jnp.int32, shape, dim)


def units_body(ff, pad, at, held, partner, mine, other, units, weight, grouped, hot_last):
    me, y, g = at[0], at[1], at[2]
    total = CHUNKS * ROWS
    a = iota((total, total), 0)
    place = ((a >> 2) & 3) * HALF + (a >> 6) * 16 + ((a >> 4) & 3) * 4 + (a & 3)
    grouped[...] = (place == iota((total, total), 1)).astype(BF16)
    p = iota((1, total), 1)
    slot = me * HALF + (p >> 6) * 16 + ((p >> 4) & 3) * 4 + (p & 3)
    group = (p >> 2) & 3
    token = token_at(slot, y)
    hot_last[...] = (token_at(iota((TOK, TOK), 0), y) == iota((TOK, TOK), 1)).astype(BF16)
    gap = jnp.zeros((pad - ff, total), F32)
    for j in range(CORE):
        moved = None
        for k in range(DP):
            wanted = jnp.where(group == ((g - k) & 3), token, -1)
            hot = (iota((TOK, total), 0) == wanted).astype(BF16)
            term = dot((held, partner)[j][k], hot, 1, 0)
            moved = term if moved is None else moved + term
        units[pl.ds(j * pad, pad)] = jnp.concatenate([moved, gap], axis=0).astype(BF16)
    blank = jnp.zeros((pad - ff, mine.shape[1]), BF16)
    weight[pl.ds(0, ff)] = mine[...]
    weight[pl.ds(ff, pad - ff)] = blank
    weight[pl.ds(pad, ff)] = other[...]
    weight[pl.ds(pad + ff, pad - ff)] = blank


def early_body(first, units, weight, grouped, *refs):
    grad, parts = refs[-2:]
    before, chunks = (refs[:2], refs[2:-2]) if first > 0 else (None, refs[:-2])
    n = len(chunks) * ROWS
    start = first * ROWS
    width = weight.shape[1]
    inner = jnp.concatenate([c[...] for c in chunks], axis=0)
    ig = dot(weight[...], inner, 1, 1).astype(BF16)
    moved = dot(ig, grouped[pl.ds(start, n)], 1, 0)
    if before:
        moved = moved + before[1][...].astype(F32)
    parts[...] = moved.astype(BF16)
    left = units[:, start:start + n]
    for j in range(0, width, 512):
        cols = jnp.concatenate([c[:, j:j + 512] for c in chunks], axis=0)
        total = dot(left, cols, 1, 0)
        grad[:, j:j + 512] = before[0][:, j:j + 512] + total if before else total


def parts_body(ff, pad, at, weight, grouped, early, *refs):
    chunks, (out,) = refs[:-1], refs[-1:]
    me = at[0]
    n = EARLY * ROWS
    inner = jnp.concatenate([c[...] for c in chunks], axis=0)
    ig = dot(weight[...], inner, 1, 1).astype(BF16)
    parts = (dot(ig, grouped[pl.ds(n, CHUNKS * ROWS - n)], 1, 0) + early[...].astype(F32)).astype(BF16)
    for g in range(DP):
        for j in range(CORE):
            out[g * CORE + (me ^ j)] = parts[j * pad:j * pad + ff, g * HALF:(g + 1) * HALF]


def late_body(ff, pad, units, grad, *refs):
    chunks, (keep, give) = refs[:-2], refs[-2:]
    n = EARLY * ROWS
    width = grad.shape[1]
    left = units[:, n:]
    for k in range(0, width, 512):
        cols = jnp.concatenate([c[:, k:k + 512] for c in chunks], axis=0)
        total = grad[:, k:k + 512] + dot(left, cols, 1, 0)
        keep[:, k:k + 512] = total[:ff]
        give[:, k:k + 512] = total[pad:pad + ff].astype(BF16)


def final_body(hot, back, out):
    halves = []
    for c in range(CORE):
        total = back[c].astype(F32)
        for g in range(1, DP):
            total = total + back[g * CORE + c].astype(F32)
        halves.append(total.astype(BF16))
    out[...] = dot(jnp.concatenate(halves, axis=1), hot[...], 1, 0).astype(BF16)


def add_body(keep, taken, out):
    out[...] = (keep[...] + taken[...].astype(F32)).astype(BF16)


def ring(value, cross=0):
    return lax.ppermute(value, ("y", "core"), ring_pairs(cross))


def step(hidden, out_grad, down_weight):
    ff, width = down_weight.shape
    pad = -(-ff // 16) * 16
    at = jnp.stack([lax.axis_index(name) for name in ("core", "y", "dp")]).astype(jnp.int32)

    row = jnp.broadcast_to(out_grad.reshape(DP, 1, 2, width // 2), (DP, ZH, 2, width // 2))
    row = row.reshape(DP * ZH, 2, width // 2)
    mine = lax.all_to_all(row, ("dp", "zh"), 0, 0, tiled=True).reshape(DP * ZH, width)
    spread = jnp.broadcast_to(mine[None], (X, DP * ZH, width))
    u0 = lax.all_to_all(spread, "x", 0, 0, tiled=True).reshape(ROWS, width)
    away = lax.ppermute(mine, "y", [(y, (y + Y // 2) % Y) for y in range(Y)])
    away = jnp.broadcast_to(away[None], (X, DP * ZH, width))
    u4 = lax.all_to_all(away, "x", 0, 0, tiled=True).reshape(ROWS, width)

    here = hidden.T
    there = []
    for k in range(1, DP):
        there.append(lax.ppermute(here, "dp", [(g, (g + k) % DP) for g in range(DP)]))
    held = jnp.stack([here] + there)
    partner = lax.ppermute(held, "core", SWAP)
    other = lax.ppermute(down_weight, "core", SWAP)
    units, weight, grouped, hot = call(
        functools.partial(units_body, ff, pad),
        [
            ((2 * pad, CHUNKS * ROWS), BF16), ((2 * pad, width), BF16),
            ((CHUNKS * ROWS, CHUNKS * ROWS), BF16), ((TOK, TOK), BF16),
        ],
        at, held, partner, down_weight, other,
    )

    u1 = ring(u0)
    v1 = ring(u0, cross=1)
    u2 = ring(u1)
    v2 = ring(v1)
    u3 = ring(u2)
    v3 = ring(v2)

    flops = 4 * pad * width * ROWS * CORE
    shapes = [((2 * pad, width), F32), ((2 * pad, CHUNKS * ROWS), BF16)]
    grad, parts = call(
        functools.partial(early_body, 0), shapes, units, weight, grouped, u0, u4, u1, v1, flops=4 * flops
    )
    grad, parts = call(
        functools.partial(early_body, 4), shapes, units, weight, grouped, grad, parts, u2, v2,
        flops=2 * flops, aliases={3: 0, 4: 1},
    )
    (parts,) = call(
        functools.partial(parts_body, ff, pad), [((DP * CORE, ff, HALF), BF16)],
        at, weight, grouped, parts, u3, v3, flops=2 * flops,
    )
    back = lax.all_to_all(parts, ("dp", "core"), 0, 0, tiled=True)
    keep, give = call(
        functools.partial(late_body, ff, pad), [((ff, width), F32), ((ff, width), BF16)],
        units, grad, u3, v3, flops=2 * flops,
    )
    taken = lax.ppermute(give, "core", SWAP)
    (weight_grad,) = call(add_body, [((ff, width), BF16)], keep, taken)
    (input_grad,) = call(final_body, [((ff, TOK), BF16)], hot, back)
    return input_grad.T, weight_grad


def solution(mesh):
    fine = Mesh(mesh.devices.reshape(DP, Y, X, ZH, CORE), ("dp", "y", "x", "zh", "core"))
    tp = ("y", "x", "zh", "core")
    return jax.shard_map(
        step,
        mesh=fine,
        in_specs=(P("dp", tp), P(("dp",) + tp, None), P(tp, "dp")),
        out_specs=(P("dp", tp), P(tp, "dp")),
        check_vma=False,
    )
```

```python
import functools

import jax
import jax.numpy as jnp
from jax import lax
from jax.experimental import pallas as pl
from jax.experimental.pallas import tpu as pltpu
from jax.sharding import Mesh, PartitionSpec as P


BF16, F32 = jnp.bfloat16, jnp.float32
DP, Y, X, ZH, CORE = 4, 8, 4, 4, 2
ROWS = X * DP * ZH
CHUNKS = 8
EARLY = 6
TOK = 256
HALF = TOK // CORE
VMEM = pl.BlockSpec(memory_space=pltpu.VMEM)
SMEM = pl.BlockSpec(memory_space=pltpu.SMEM)
SWAP = [(0, 1), (1, 0)]


def ring_pairs(cross):
    pairs = []
    for y in range(Y):
        for core, way in ((0, 1), (1, -1)):
            pairs.append((y * CORE + (core ^ cross), ((y + way) % Y) * CORE + core))
    return pairs


def dot(a, b, ca, cb):
    return lax.dot_general(a, b, (((ca,), (cb,)), ((), ())), preferred_element_type=F32)


def call(body, outs, *args, flops=0):
    outs = [jax.ShapeDtypeStruct(s, d) for s, d in outs]
    moved = sum(a.size * a.dtype.itemsize for a in args) + sum(o.size * o.dtype.itemsize for o in outs)
    specs = [SMEM if a.dtype == jnp.int32 else VMEM for a in args]
    return pl.pallas_call(
        body,
        out_shape=outs,
        in_specs=specs,
        out_specs=[VMEM] * len(outs),
        cost_estimate=pl.CostEstimate(flops=flops, bytes_accessed=moved, transcendentals=0),
        compiler_params=pltpu.CompilerParams(vmem_limit_bytes=12 * 2**20),
    )(*args)


def token_at(p, y):
    core, q, x, zh = p >> 7, (p >> 4) & 7, (p >> 2) & 3, p & 3
    step = jnp.where(q == 1, 4, q >> 1)
    flip = jnp.where(q == 1, 0, q & 1)
    row = (y + jnp.where(core == 0, -step, step)) & 7
    return row * 32 + x * 8 + zh * 2 + (core ^ flip)


def iota(shape, dim):
    return lax.broadcasted_iota(jnp.int32, shape, dim)


def units_body(ff, pad, at, held, partner, mine, other, units, weight, grouped, hot_last):
    me, y, g = at[0], at[1], at[2]
    total = CHUNKS * ROWS
    a = iota((total, total), 0)
    place = ((a >> 2) & 3) * HALF + (a >> 6) * 16 + ((a >> 4) & 3) * 4 + (a & 3)
    grouped[...] = (place == iota((total, total), 1)).astype(BF16)
    p = iota((1, total), 1)
    slot = me * HALF + (p >> 6) * 16 + ((p >> 4) & 3) * 4 + (p & 3)
    group = (p >> 2) & 3
    token = token_at(slot, y)
    hot_last[...] = (token_at(iota((TOK, TOK), 0), y) == iota((TOK, TOK), 1)).astype(BF16)
    gap = jnp.zeros((pad - ff, total), F32)
    for j in range(CORE):
        moved = None
        for k in range(DP):
            wanted = jnp.where(group == ((g - k) & 3), token, -1)
            hot = (iota((TOK, total), 0) == wanted).astype(BF16)
            term = dot((held, partner)[j][k], hot, 1, 0)
            moved = term if moved is None else moved + term
        units[pl.ds(j * pad, pad)] = jnp.concatenate([moved, gap], axis=0).astype(BF16)
    blank = jnp.zeros((pad - ff, mine.shape[1]), BF16)
    weight[pl.ds(0, ff)] = mine[...]
    weight[pl.ds(ff, pad - ff)] = blank
    weight[pl.ds(pad, ff)] = other[...]
    weight[pl.ds(pad + ff, pad - ff)] = blank


def early_body(units, weight, grouped, *refs):
    chunks, (grad, parts) = refs[:EARLY], refs[EARLY:]
    n = EARLY * ROWS
    width = weight.shape[1]
    inner = jnp.concatenate([c[...] for c in chunks], axis=0)
    ig = dot(weight[...], inner, 1, 1).astype(BF16)
    parts[...] = dot(ig, grouped[pl.ds(0, n)], 1, 0).astype(BF16)
    left = units[:, :n]
    for j in range(0, width, 512):
        cols = jnp.concatenate([c[:, j:j + 512] for c in chunks], axis=0)
        grad[:, j:j + 512] = dot(left, cols, 1, 0)


def parts_body(ff, pad, at, weight, grouped, early, *refs):
    chunks, (out,) = refs[:-1], refs[-1:]
    me = at[0]
    n = EARLY * ROWS
    inner = jnp.concatenate([c[...] for c in chunks], axis=0)
    ig = dot(weight[...], inner, 1, 1).astype(BF16)
    parts = (dot(ig, grouped[pl.ds(n, CHUNKS * ROWS - n)], 1, 0) + early[...].astype(F32)).astype(BF16)
    for g in range(DP):
        for j in range(CORE):
            out[g * CORE + (me ^ j)] = parts[j * pad:j * pad + ff, g * HALF:(g + 1) * HALF]


def late_body(ff, pad, units, grad, *refs):
    chunks, (keep, give) = refs[:-2], refs[-2:]
    n = EARLY * ROWS
    width = grad.shape[1]
    left = units[:, n:]
    for k in range(0, width, 512):
        cols = jnp.concatenate([c[:, k:k + 512] for c in chunks], axis=0)
        total = grad[:, k:k + 512] + dot(left, cols, 1, 0)
        keep[:, k:k + 512] = total[:ff]
        give[:, k:k + 512] = total[pad:pad + ff].astype(BF16)


def final_body(hot, back, out):
    halves = []
    for c in range(CORE):
        total = back[c].astype(F32)
        for g in range(1, DP):
            total = total + back[g * CORE + c].astype(F32)
        halves.append(total.astype(BF16))
    out[...] = dot(jnp.concatenate(halves, axis=1), hot[...], 1, 0).astype(BF16)


def add_body(keep, taken, out):
    out[...] = (keep[...] + taken[...].astype(F32)).astype(BF16)


def ring(value, cross=0):
    return lax.ppermute(value, ("y", "core"), ring_pairs(cross))


def step(hidden, out_grad, down_weight):
    ff, width = down_weight.shape
    pad = -(-ff // 16) * 16
    at = jnp.stack([lax.axis_index(name) for name in ("core", "y", "dp")]).astype(jnp.int32)

    row = jnp.broadcast_to(out_grad.reshape(DP, 1, 2, width // 2), (DP, ZH, 2, width // 2))
    row = row.reshape(DP * ZH, 2, width // 2)
    row, at = lax.optimization_barrier((row, at))
    mine = lax.all_to_all(row, ("dp", "zh"), 0, 0, tiled=True).reshape(DP * ZH, width)
    spread = jnp.broadcast_to(mine[None], (X, DP * ZH, width))
    u0 = lax.all_to_all(spread, "x", 0, 0, tiled=True).reshape(ROWS, width)
    away = lax.ppermute(mine, "y", [(y, (y + Y // 2) % Y) for y in range(Y)])
    away = jnp.broadcast_to(away[None], (X, DP * ZH, width))
    u4 = lax.all_to_all(away, "x", 0, 0, tiled=True).reshape(ROWS, width)

    here = hidden.T
    there = []
    for k in range(1, DP):
        there.append(lax.ppermute(here, "dp", [(g, (g + k) % DP) for g in range(DP)]))
    held = jnp.stack([here] + there)
    partner = lax.ppermute(held, "core", SWAP)
    other = lax.ppermute(down_weight, "core", SWAP)
    units, weight, grouped, hot = call(
        functools.partial(units_body, ff, pad),
        [
            ((2 * pad, CHUNKS * ROWS), BF16), ((2 * pad, width), BF16),
            ((CHUNKS * ROWS, CHUNKS * ROWS), BF16), ((TOK, TOK), BF16),
        ],
        at, held, partner, down_weight, other,
    )

    u1 = ring(u0)
    v1 = ring(u0, cross=1)
    u2 = ring(u1)
    v2 = ring(v1)
    u3 = ring(u2)
    v3 = ring(v2)

    flops = 4 * pad * width * ROWS * CORE
    shapes = [((2 * pad, width), F32), ((2 * pad, CHUNKS * ROWS), BF16)]
    grad, parts = call(
        early_body, shapes, units, weight, grouped, u0, u4, u1, v1, u2, v2, flops=EARLY * flops
    )
    (parts,) = call(
        functools.partial(parts_body, ff, pad), [((DP * CORE, ff, HALF), BF16)],
        at, weight, grouped, parts, u3, v3, flops=2 * flops,
    )
    back = lax.all_to_all(parts, ("dp", "core"), 0, 0, tiled=True)
    keep, give = call(
        functools.partial(late_body, ff, pad), [((ff, width), F32), ((ff, width), BF16)],
        units, grad, u3, v3, flops=2 * flops,
    )
    taken = lax.ppermute(give, "core", SWAP)
    (weight_grad,) = call(add_body, [((ff, width), BF16)], keep, taken)
    (input_grad,) = call(final_body, [((ff, TOK), BF16)], hot, back)
    return input_grad.T, weight_grad


def solution(mesh):
    fine = Mesh(mesh.devices.reshape(DP, Y, X, ZH, CORE), ("dp", "y", "x", "zh", "core"))
    tp = ("y", "x", "zh", "core")
    return jax.shard_map(
        step,
        mesh=fine,
        in_specs=(P("dp", tp), P(("dp",) + tp, None), P(tp, "dp")),
        out_specs=(P("dp", tp), P(tp, "dp")),
        check_vma=False,
    )
```

```python
import functools

import jax
import jax.numpy as jnp
from jax import lax
from jax.experimental import pallas as pl
from jax.experimental.pallas import tpu as pltpu
from jax.sharding import Mesh, PartitionSpec as P


BF16, F32 = jnp.bfloat16, jnp.float32
DP, Y, X, ZH, CORE = 4, 8, 4, 4, 2
ROWS = X * DP * ZH
CHUNKS = 8
EARLY = 6
TOK = 256
HALF = TOK // CORE
VMEM = pl.BlockSpec(memory_space=pltpu.VMEM)
SMEM = pl.BlockSpec(memory_space=pltpu.SMEM)
SWAP = [(0, 1), (1, 0)]


def ring_pairs(cross):
    pairs = []
    for y in range(Y):
        for core, way in ((0, 1), (1, -1)):
            pairs.append((y * CORE + (core ^ cross), ((y + way) % Y) * CORE + core))
    return pairs


def dot(a, b, ca, cb):
    return lax.dot_general(a, b, (((ca,), (cb,)), ((), ())), preferred_element_type=F32)


def call(body, outs, *args, flops=0):
    outs = [jax.ShapeDtypeStruct(s, d) for s, d in outs]
    moved = sum(a.size * a.dtype.itemsize for a in args) + sum(o.size * o.dtype.itemsize for o in outs)
    specs = [SMEM if a.dtype == jnp.int32 else VMEM for a in args]
    return pl.pallas_call(
        body,
        out_shape=outs,
        in_specs=specs,
        out_specs=[VMEM] * len(outs),
        cost_estimate=pl.CostEstimate(flops=flops, bytes_accessed=moved, transcendentals=0),
        compiler_params=pltpu.CompilerParams(vmem_limit_bytes=12 * 2**20),
    )(*args)


def token_at(p, y):
    core, q, x, zh = p >> 7, (p >> 4) & 7, (p >> 2) & 3, p & 3
    step = jnp.where(q == 1, 4, q >> 1)
    flip = jnp.where(q == 1, 0, q & 1)
    row = (y + jnp.where(core == 0, -step, step)) & 7
    return row * 32 + x * 8 + zh * 2 + (core ^ flip)


def iota(shape, dim):
    return lax.broadcasted_iota(jnp.int32, shape, dim)


def units_body(ff, pad, at, held, partner, units, weight, grouped, hot_last):
    me, y, g = at[0], at[1], at[2]
    total = CHUNKS * ROWS
    width = weight.shape[1]
    a = iota((total, total), 0)
    place = ((a >> 2) & 3) * HALF + (a >> 6) * 16 + ((a >> 4) & 3) * 4 + (a & 3)
    grouped[...] = (place == iota((total, total), 1)).astype(BF16)
    hot_last[...] = (token_at(iota((TOK, TOK), 0), y) == iota((TOK, TOK), 1)).astype(BF16)
    p = iota((1, total), 1)
    token = token_at(me * HALF + (p >> 6) * 16 + ((p >> 4) & 3) * 4 + (p & 3), y)
    wanted = ((g - ((p >> 2) & 3)) & 3) * TOK + token
    hot = (iota((DP * TOK, total), 0) == wanted).astype(BF16)
    gap = jnp.zeros((pad - ff, total), F32)
    blank = jnp.zeros((pad - ff, width), BF16)
    for j, source in enumerate((held, partner)):
        moved = dot(source[:, width:], hot, 1, 0)
        units[pl.ds(j * pad, pad)] = jnp.concatenate([moved, gap], axis=0).astype(BF16)
        row = pl.multiple_of((me ^ j) * pad, 16)
        weight[pl.ds(row, ff)] = source[:, :width]
        weight[pl.ds(row + ff, pad - ff)] = blank


def early_body(units, weight, grouped, *refs):
    chunks, (grad, parts) = refs[:EARLY], refs[EARLY:]
    n = EARLY * ROWS
    width = weight.shape[1]
    inner = jnp.concatenate([c[...] for c in chunks], axis=0)
    ig = dot(weight[...], inner, 1, 1).astype(BF16)
    parts[...] = dot(ig, grouped[pl.ds(0, n)], 1, 0).astype(BF16)
    left = units[:, :n]
    for j in range(0, width, 512):
        cols = jnp.concatenate([c[:, j:j + 512] for c in chunks], axis=0)
        grad[:, j:j + 512] = dot(left, cols, 1, 0)


def parts_body(ff, pad, weight, grouped, early, *refs):
    chunks, (out,) = refs[:-1], refs[-1:]
    n = EARLY * ROWS
    inner = jnp.concatenate([c[...] for c in chunks], axis=0)
    ig = dot(weight[...], inner, 1, 1).astype(BF16)
    parts = (dot(ig, grouped[pl.ds(n, CHUNKS * ROWS - n)], 1, 0) + early[...].astype(F32)).astype(BF16)
    for g in range(DP):
        for j in range(CORE):
            out[g * CORE + j] = parts[j * pad:j * pad + ff, g * HALF:(g + 1) * HALF]


def late_body(ff, pad, units, grad, *refs):
    chunks, (keep, give) = refs[:-2], refs[-2:]
    n = EARLY * ROWS
    width = grad.shape[1]
    left = units[:, n:]
    for k in range(0, width, 512):
        cols = jnp.concatenate([c[:, k:k + 512] for c in chunks], axis=0)
        total = grad[:, k:k + 512] + dot(left, cols, 1, 0)
        keep[:, k:k + 512] = total[:ff]
        give[:, k:k + 512] = total[pad:pad + ff].astype(BF16)


def final_body(hot, back, out):
    halves = []
    for c in range(CORE):
        total = back[c].astype(F32)
        for g in range(1, DP):
            total = total + back[g * CORE + c].astype(F32)
        halves.append(total.astype(BF16))
    out[...] = dot(jnp.concatenate(halves, axis=1), hot[...], 1, 0).astype(BF16)


def add_body(keep, taken, out):
    out[...] = (keep[...] + taken[...].astype(F32)).astype(BF16)


def ring(value, cross=0):
    return lax.ppermute(value, ("y", "core"), ring_pairs(cross))


def step(hidden, out_grad, down_weight):
    ff, width = down_weight.shape
    pad = -(-ff // 16) * 16
    at = jnp.stack([lax.axis_index(name) for name in ("core", "y", "dp")]).astype(jnp.int32)

    row = jnp.broadcast_to(out_grad.reshape(DP, 1, 2, width // 2), (DP, ZH, 2, width // 2))
    row = row.reshape(DP * ZH, 2, width // 2)
    row, at = lax.optimization_barrier((row, at))
    mine = lax.all_to_all(row, ("dp", "zh"), 0, 0, tiled=True).reshape(DP * ZH, width)
    spread = jnp.broadcast_to(mine[None], (X, DP * ZH, width))
    u0 = lax.all_to_all(spread, "x", 0, 0, tiled=True).reshape(ROWS, width)
    away = lax.ppermute(mine, "y", [(y, (y + Y // 2) % Y) for y in range(Y)])
    away = jnp.broadcast_to(away[None], (X, DP * ZH, width))
    u4 = lax.all_to_all(away, "x", 0, 0, tiled=True).reshape(ROWS, width)

    here = hidden.T
    there = []
    for k in range(1, DP):
        there.append(lax.ppermute(here, "dp", [(g, (g + k) % DP) for g in range(DP)]))
    held = jnp.concatenate([down_weight, here] + there, axis=1)
    partner = lax.ppermute(held, "core", SWAP)
    units, weight, grouped, hot = call(
        functools.partial(units_body, ff, pad),
        [
            ((2 * pad, CHUNKS * ROWS), BF16), ((2 * pad, width), BF16),
            ((CHUNKS * ROWS, CHUNKS * ROWS), BF16), ((TOK, TOK), BF16),
        ],
        at, held, partner,
    )

    u1 = ring(u0)
    v1 = ring(u0, cross=1)
    u2 = ring(u1)
    v2 = ring(v1)
    u3 = ring(u2)
    v3 = ring(v2)

    flops = 4 * pad * width * ROWS * CORE
    shapes = [((2 * pad, width), F32), ((2 * pad, CHUNKS * ROWS), BF16)]
    grad, parts = call(
        early_body, shapes, units, weight, grouped, u0, u4, u1, v1, u2, v2, flops=EARLY * flops
    )
    (parts,) = call(
        functools.partial(parts_body, ff, pad), [((DP * CORE, ff, HALF), BF16)],
        weight, grouped, parts, u3, v3, flops=2 * flops,
    )
    back = lax.all_to_all(parts, ("dp", "core"), 0, 0, tiled=True)
    keep, give = call(
        functools.partial(late_body, ff, pad), [((ff, width), F32), ((ff, width), BF16)],
        units, grad, u3, v3, flops=2 * flops,
    )
    taken = lax.ppermute(give, "core", SWAP)
    (weight_grad,) = call(add_body, [((ff, width), BF16)], keep, taken)
    (input_grad,) = call(final_body, [((ff, TOK), BF16)], hot, back)
    return input_grad.T, weight_grad


def solution(mesh):
    fine = Mesh(mesh.devices.reshape(DP, Y, X, ZH, CORE), ("dp", "y", "x", "zh", "core"))
    tp = ("y", "x", "zh", "core")
    return jax.shard_map(
        step,
        mesh=fine,
        in_specs=(P("dp", tp), P(("dp",) + tp, None), P(tp, "dp")),
        out_specs=(P("dp", tp), P(tp, "dp")),
        check_vma=False,
    )
```

```python
import functools

import jax
import jax.numpy as jnp
from jax import lax
from jax.experimental import pallas as pl
from jax.experimental.pallas import tpu as pltpu
from jax.sharding import Mesh, PartitionSpec as P


BF16, F32 = jnp.bfloat16, jnp.float32
DP, Y, X, ZH, CORE = 4, 8, 4, 4, 2
ROWS = X * DP * ZH
CHUNKS = 8
EARLY = 6
TOK = 256
HALF = TOK // CORE
VMEM = pl.BlockSpec(memory_space=pltpu.VMEM)
SMEM = pl.BlockSpec(memory_space=pltpu.SMEM)
SWAP = [(0, 1), (1, 0)]


def ring_pairs(cross):
    pairs = []
    for y in range(Y):
        for core, way in ((0, 1), (1, -1)):
            pairs.append((y * CORE + (core ^ cross), ((y + way) % Y) * CORE + core))
    return pairs


def dot(a, b, ca, cb):
    return lax.dot_general(a, b, (((ca,), (cb,)), ((), ())), preferred_element_type=F32)


def call(body, outs, *args, flops=0):
    outs = [jax.ShapeDtypeStruct(s, d) for s, d in outs]
    moved = sum(a.size * a.dtype.itemsize for a in args) + sum(o.size * o.dtype.itemsize for o in outs)
    specs = [SMEM if a.dtype == jnp.int32 else VMEM for a in args]
    return pl.pallas_call(
        body,
        out_shape=outs,
        in_specs=specs,
        out_specs=[VMEM] * len(outs),
        cost_estimate=pl.CostEstimate(flops=flops, bytes_accessed=moved, transcendentals=0),
        compiler_params=pltpu.CompilerParams(vmem_limit_bytes=12 * 2**20),
    )(*args)


def token_at(p, y):
    core, q, x, zh = p >> 7, (p >> 4) & 7, (p >> 2) & 3, p & 3
    step = jnp.where(q == 1, 4, q >> 1)
    flip = jnp.where(q == 1, 0, q & 1)
    row = (y + jnp.where(core == 0, -step, step)) & 7
    return row * 32 + x * 8 + zh * 2 + (core ^ flip)


def iota(shape, dim):
    return lax.broadcasted_iota(jnp.int32, shape, dim)


def units_body(ff, pad, at, held, partner, units, weight, grouped, hot_last):
    me, y, g = at[0], at[1], at[2]
    total = CHUNKS * ROWS
    width = weight.shape[1]
    a = iota((total, total), 0)
    place = ((a >> 2) & 3) * HALF + (a >> 6) * 16 + ((a >> 4) & 3) * 4 + (a & 3)
    grouped[...] = (place == iota((total, total), 1)).astype(BF16)
    hot_last[...] = (token_at(iota((TOK, TOK), 0), y) == iota((TOK, TOK), 1)).astype(BF16)
    p = iota((1, total), 1)
    token = token_at(me * HALF + (p >> 6) * 16 + ((p >> 4) & 3) * 4 + (p & 3), y)
    wanted = ((g - ((p >> 2) & 3)) & 3) * TOK + token
    hot = (iota((DP * TOK, total), 0) == wanted).astype(BF16)
    gap = jnp.zeros((pad - ff, total), F32)
    blank = jnp.zeros((pad - ff, width), BF16)
    for j, source in enumerate((held, partner)):
        moved = dot(source[:, width:], hot, 1, 0)
        units[pl.ds(j * pad, pad)] = jnp.concatenate([moved, gap], axis=0).astype(BF16)
        row = pl.multiple_of((me ^ j) * pad, 16)
        weight[pl.ds(row, ff)] = source[:, :width]
        weight[pl.ds(row + ff, pad - ff)] = blank


def early_body(weight, grouped, *refs):
    chunks, (parts,) = refs[:-1], refs[-1:]
    inner = jnp.concatenate([c[...] for c in chunks], axis=0)
    ig = dot(weight[...], inner, 1, 1).astype(BF16)
    parts[...] = dot(ig, grouped[pl.ds(0, EARLY * ROWS)], 1, 0).astype(BF16)


def parts_body(ff, pad, weight, grouped, early, *refs):
    chunks, (out,) = refs[:-1], refs[-1:]
    n = EARLY * ROWS
    inner = jnp.concatenate([c[...] for c in chunks], axis=0)
    ig = dot(weight[...], inner, 1, 1).astype(BF16)
    parts = (dot(ig, grouped[pl.ds(n, CHUNKS * ROWS - n)], 1, 0) + early[...].astype(F32)).astype(BF16)
    for g in range(DP):
        for j in range(CORE):
            out[g * CORE + j] = parts[j * pad:j * pad + ff, g * HALF:(g + 1) * HALF]


def grad_body(ff, pad, units, *refs):
    chunks, (keep, give) = refs[:-2], refs[-2:]
    left = units[...]
    for k in range(0, give.shape[1], 512):
        cols = jnp.concatenate([c[:, k:k + 512] for c in chunks], axis=0)
        total = dot(left, cols, 1, 0)
        keep[:, k:k + 512] = total[:ff]
        give[:, k:k + 512] = total[pad:pad + ff].astype(BF16)


def final_body(hot, back, out):
    halves = []
    for c in range(CORE):
        total = back[c].astype(F32)
        for g in range(1, DP):
            total = total + back[g * CORE + c].astype(F32)
        halves.append(total.astype(BF16))
    out[...] = dot(jnp.concatenate(halves, axis=1), hot[...], 1, 0).astype(BF16)


def add_body(keep, taken, out):
    out[...] = (keep[...] + taken[...].astype(F32)).astype(BF16)


def ring(value, cross=0):
    return lax.ppermute(value, ("y", "core"), ring_pairs(cross))


def step(hidden, out_grad, down_weight):
    ff, width = down_weight.shape
    pad = -(-ff // 16) * 16
    at = jnp.stack([lax.axis_index(name) for name in ("core", "y", "dp")]).astype(jnp.int32)

    row = jnp.broadcast_to(out_grad.reshape(DP, 1, 2, width // 2), (DP, ZH, 2, width // 2))
    row = row.reshape(DP * ZH, 2, width // 2)
    row, at = lax.optimization_barrier((row, at))
    mine = lax.all_to_all(row, ("dp", "zh"), 0, 0, tiled=True).reshape(DP * ZH, width)
    spread = jnp.broadcast_to(mine[None], (X, DP * ZH, width))
    u0 = lax.all_to_all(spread, "x", 0, 0, tiled=True).reshape(ROWS, width)
    away = lax.ppermute(mine, "y", [(y, (y + Y // 2) % Y) for y in range(Y)])
    away = jnp.broadcast_to(away[None], (X, DP * ZH, width))
    u4 = lax.all_to_all(away, "x", 0, 0, tiled=True).reshape(ROWS, width)

    here = hidden.T
    there = []
    for k in range(1, DP):
        there.append(lax.ppermute(here, "dp", [(g, (g + k) % DP) for g in range(DP)]))
    *pieces, _ = lax.optimization_barrier((down_weight, here, *there, u0))
    held = jnp.concatenate(pieces, axis=1)
    partner = lax.ppermute(held, "core", SWAP)
    units, weight, grouped, hot = call(
        functools.partial(units_body, ff, pad),
        [
            ((2 * pad, CHUNKS * ROWS), BF16), ((2 * pad, width), BF16),
            ((CHUNKS * ROWS, CHUNKS * ROWS), BF16), ((TOK, TOK), BF16),
        ],
        at, held, partner,
    )

    u1 = ring(u0)
    v1 = ring(u0, cross=1)
    u2 = ring(u1)
    v2 = ring(v1)
    u3 = ring(u2)
    v3 = ring(v2)

    flops = 2 * pad * width * ROWS * CORE
    (parts,) = call(
        early_body, [((2 * pad, CHUNKS * ROWS), BF16)], weight, grouped, u0, u4, u1, v1, u2, v2, flops=EARLY * flops
    )
    (parts,) = call(
        functools.partial(parts_body, ff, pad), [((DP * CORE, ff, HALF), BF16)],
        weight, grouped, parts, u3, v3, flops=2 * flops,
    )
    back = lax.all_to_all(parts, ("dp", "core"), 0, 0, tiled=True)
    keep, give = call(
        functools.partial(grad_body, ff, pad), [((ff, width), F32), ((ff, width), BF16)],
        units, u0, u4, u1, v1, u2, v2, u3, v3, flops=CHUNKS * flops,
    )
    taken = lax.ppermute(give, "core", SWAP)
    (weight_grad,) = call(add_body, [((ff, width), BF16)], keep, taken)
    (input_grad,) = call(final_body, [((ff, TOK), BF16)], hot, back)
    return input_grad.T, weight_grad


def solution(mesh):
    fine = Mesh(mesh.devices.reshape(DP, Y, X, ZH, CORE), ("dp", "y", "x", "zh", "core"))
    tp = ("y", "x", "zh", "core")
    return jax.shard_map(
        step,
        mesh=fine,
        in_specs=(P("dp", tp), P(("dp",) + tp, None), P(tp, "dp")),
        out_specs=(P("dp", tp), P(tp, "dp")),
        check_vma=False,
    )
```

```python
import functools

import jax
import jax.numpy as jnp
from jax import lax
from jax.experimental import pallas as pl
from jax.experimental.pallas import tpu as pltpu
from jax.sharding import Mesh, PartitionSpec as P


BF16, F32 = jnp.bfloat16, jnp.float32
DP, Y, X, ZH, CORE = 4, 8, 4, 4, 2
ROWS = X * DP * ZH
CHUNKS = 8
EARLY = 6
TOK = 256
HALF = TOK // CORE
VMEM = pl.BlockSpec(memory_space=pltpu.VMEM)
SMEM = pl.BlockSpec(memory_space=pltpu.SMEM)
SWAP = [(0, 1), (1, 0)]


def ring_pairs(cross):
    pairs = []
    for y in range(Y):
        for core, way in ((0, 1), (1, -1)):
            pairs.append((y * CORE + (core ^ cross), ((y + way) % Y) * CORE + core))
    return pairs


def dot(a, b, ca, cb):
    return lax.dot_general(a, b, (((ca,), (cb,)), ((), ())), preferred_element_type=F32)


def call(body, outs, *args, flops=0):
    outs = [jax.ShapeDtypeStruct(s, d) for s, d in outs]
    moved = sum(a.size * a.dtype.itemsize for a in args) + sum(o.size * o.dtype.itemsize for o in outs)
    specs = [SMEM if a.dtype == jnp.int32 else VMEM for a in args]
    return pl.pallas_call(
        body,
        out_shape=outs,
        in_specs=specs,
        out_specs=[VMEM] * len(outs),
        cost_estimate=pl.CostEstimate(flops=flops, bytes_accessed=moved, transcendentals=0),
        compiler_params=pltpu.CompilerParams(vmem_limit_bytes=12 * 2**20),
    )(*args)


def token_at(p, y):
    core, q, x, zh = p >> 7, (p >> 4) & 7, (p >> 2) & 3, p & 3
    step = jnp.where(q == 1, 4, q >> 1)
    flip = jnp.where(q == 1, 0, q & 1)
    row = (y + jnp.where(core == 0, -step, step)) & 7
    return row * 32 + x * 8 + zh * 2 + (core ^ flip)


def iota(shape, dim):
    return lax.broadcasted_iota(jnp.int32, shape, dim)


def units_body(ff, pad, at, held, partner, units, weight, grouped, hot_last):
    me, y, g = at[0], at[1], at[2]
    total = CHUNKS * ROWS
    width = weight.shape[1]
    a = iota((total, total), 0)
    place = ((a >> 2) & 3) * HALF + (a >> 6) * 16 + ((a >> 4) & 3) * 4 + (a & 3)
    grouped[...] = (place == iota((total, total), 1)).astype(BF16)
    hot_last[...] = (token_at(iota((TOK, TOK), 0), y) == iota((TOK, TOK), 1)).astype(BF16)
    p = iota((1, total), 1)
    token = token_at(me * HALF + (p >> 6) * 16 + ((p >> 4) & 3) * 4 + (p & 3), y)
    wanted = (g ^ ((p >> 2) & 3)) * TOK + token
    hot = (iota((DP * TOK, total), 0) == wanted).astype(BF16)
    gap = jnp.zeros((pad - ff, total), F32)
    blank = jnp.zeros((pad - ff, width), BF16)
    for j, source in enumerate((held, partner)):
        moved = dot(source[:, width:], hot, 1, 0)
        units[pl.ds(j * pad, pad)] = jnp.concatenate([moved, gap], axis=0).astype(BF16)
        row = pl.multiple_of((me ^ j) * pad, 16)
        weight[pl.ds(row, ff)] = source[:, :width]
        weight[pl.ds(row + ff, pad - ff)] = blank


def early_body(weight, grouped, *refs):
    chunks, (parts,) = refs[:-1], refs[-1:]
    inner = jnp.concatenate([c[...] for c in chunks], axis=0)
    ig = dot(weight[...], inner, 1, 1).astype(BF16)
    parts[...] = dot(ig, grouped[pl.ds(0, EARLY * ROWS)], 1, 0).astype(BF16)


def parts_body(ff, pad, weight, grouped, early, *refs):
    chunks, (out,) = refs[:-1], refs[-1:]
    n = EARLY * ROWS
    inner = jnp.concatenate([c[...] for c in chunks], axis=0)
    ig = dot(weight[...], inner, 1, 1).astype(BF16)
    parts = (dot(ig, grouped[pl.ds(n, CHUNKS * ROWS - n)], 1, 0) + early[...].astype(F32)).astype(BF16)
    for g in range(DP):
        for j in range(CORE):
            out[g * CORE + j] = parts[j * pad:j * pad + ff, g * HALF:(g + 1) * HALF]


def grad_body(ff, pad, units, *refs):
    chunks, (keep, give) = refs[:-2], refs[-2:]
    left = units[...]
    for k in range(0, give.shape[1], 512):
        cols = jnp.concatenate([c[:, k:k + 512] for c in chunks], axis=0)
        total = dot(left, cols, 1, 0)
        keep[:, k:k + 512] = total[:ff]
        give[:, k:k + 512] = total[pad:pad + ff].astype(BF16)


def final_body(hot, back, out):
    halves = []
    for c in range(CORE):
        total = back[c].astype(F32)
        for g in range(1, DP):
            total = total + back[g * CORE + c].astype(F32)
        halves.append(total.astype(BF16))
    out[...] = dot(jnp.concatenate(halves, axis=1), hot[...], 1, 0).astype(BF16)


def add_body(keep, taken, out):
    out[...] = (keep[...] + taken[...].astype(F32)).astype(BF16)


def ring(value, cross=0):
    return lax.ppermute(value, ("y", "core"), ring_pairs(cross))


def step(hidden, out_grad, down_weight):
    ff, width = down_weight.shape
    pad = -(-ff // 16) * 16
    at = jnp.stack([lax.axis_index(name) for name in ("core", "y", "dp")]).astype(jnp.int32)

    row = jnp.broadcast_to(out_grad.reshape(DP, 1, 2, width // 2), (DP, ZH, 2, width // 2))
    row = row.reshape(DP * ZH, 2, width // 2)
    row, at = lax.optimization_barrier((row, at))
    mine = lax.all_to_all(row, ("dp", "zh"), 0, 0, tiled=True).reshape(DP * ZH, width)
    spread = jnp.broadcast_to(mine[None], (X, DP * ZH, width))
    u0 = lax.all_to_all(spread, "x", 0, 0, tiled=True).reshape(ROWS, width)
    away = lax.ppermute(mine, "y", [(y, (y + Y // 2) % Y) for y in range(Y)])
    away = jnp.broadcast_to(away[None], (X, DP * ZH, width))
    u4 = lax.all_to_all(away, "x", 0, 0, tiled=True).reshape(ROWS, width)

    here = hidden.T
    one = lax.ppermute(here, "dp", [(g, g ^ 1) for g in range(DP)])
    two = lax.ppermute(jnp.concatenate([here, one], axis=1), "dp", [(g, g ^ 2) for g in range(DP)])
    *pieces, _ = lax.optimization_barrier((down_weight, here, one, two, u0))
    held = jnp.concatenate(pieces, axis=1)
    partner = lax.ppermute(held, "core", SWAP)
    units, weight, grouped, hot = call(
        functools.partial(units_body, ff, pad),
        [
            ((2 * pad, CHUNKS * ROWS), BF16), ((2 * pad, width), BF16),
            ((CHUNKS * ROWS, CHUNKS * ROWS), BF16), ((TOK, TOK), BF16),
        ],
        at, held, partner,
    )

    u1 = ring(u0)
    v1 = ring(u0, cross=1)
    u2 = ring(u1)
    v2 = ring(v1)
    u3 = ring(u2)
    v3 = ring(v2)

    flops = 2 * pad * width * ROWS * CORE
    (parts,) = call(
        early_body, [((2 * pad, CHUNKS * ROWS), BF16)], weight, grouped, u0, u4, u1, v1, u2, v2, flops=EARLY * flops
    )
    (parts,) = call(
        functools.partial(parts_body, ff, pad), [((DP * CORE, ff, HALF), BF16)],
        weight, grouped, parts, u3, v3, flops=2 * flops,
    )
    back = lax.all_to_all(parts, ("dp", "core"), 0, 0, tiled=True)
    keep, give = call(
        functools.partial(grad_body, ff, pad), [((ff, width), F32), ((ff, width), BF16)],
        units, u0, u4, u1, v1, u2, v2, u3, v3, flops=CHUNKS * flops,
    )
    taken = lax.ppermute(give, "core", SWAP)
    (weight_grad,) = call(add_body, [((ff, width), BF16)], keep, taken)
    (input_grad,) = call(final_body, [((ff, TOK), BF16)], hot, back)
    return input_grad.T, weight_grad


def solution(mesh):
    fine = Mesh(mesh.devices.reshape(DP, Y, X, ZH, CORE), ("dp", "y", "x", "zh", "core"))
    tp = ("y", "x", "zh", "core")
    return jax.shard_map(
        step,
        mesh=fine,
        in_specs=(P("dp", tp), P(("dp",) + tp, None), P(tp, "dp")),
        out_specs=(P("dp", tp), P(tp, "dp")),
        check_vma=False,
    )
```
